256 devices in a mesh: grp: 32 (over z_lo, x, core), shard: 8 (over z_hi, y).
Axes of the slice: x: 4, y: 4, z: 8 (z_hi: 2, z_lo: 4; z = z_hi * 4 + z_lo), core: 2. Of those that a mesh axis runs over, the one named last changes fastest.
Arguments:
- tokens: bfloat16 [16384, 2560], P(('grp', 'shard')), may hold values from -0.125 to 0.125
- target: bfloat16 [16384, 13824], P('grp', 'shard'), may hold values from -6 to 6
- post_mean: float32 [2560, 13824], P('grp', 'shard'), may hold values from -5 to 5
- post_hess: float32 [2560, 13824], P('grp', 'shard'), may hold values from 0.05 to 0.5
- weight_noise: bfloat16 [32, 2560, 13824], P(None, 'grp', 'shard'), may hold values from -6 to 6
Outputs:
- new_mean: float32 [2560, 13824], P('grp', 'shard')
- new_hess: float32 [2560, 13824], P('grp', 'shard')
The draws below stay inside these ranges and needn't reach their ends.
All inputs are finite; a program needn't handle non-finite values.
Results may differ from the reference program's by a relative error of at most 0.0018.
Values may be sent and summed in bfloat16 or wider, within the bound.
A program may use at most 192 MiB of HBM per device.

```python
import math
import jax
import jax.numpy as jnp
from jax import lax

D = 2560
FF = 13824
TOK_GRP = 512
GROUPS = 32
TOKENS = 16384


def shard_levels(rng, extent, split, low, largest):
    factor_of = 1.0
    for axis_at, parts in split:
        steps = jax.random.uniform(jax.random.fold_in(jax.random.fold_in(rng, 6), axis_at), (parts,), jnp.float32, low / len(split), largest / len(split))
        factor_of = factor_of * jnp.repeat(jnp.exp(steps), extent[axis_at] // parts).reshape((-1,) + (1,) * (len(extent) - 1 - axis_at))
    return factor_of


def noise(stream_key, shape, width, limit, pieces=(), dtype=jnp.bfloat16):
    gain = shard_levels(stream_key, shape, pieces, -0.22, 0.18) if pieces else 1.0
    result = jax.random.normal(stream_key, shape, jnp.float32) * width * gain
    return jnp.minimum(jnp.maximum(result, -limit), limit).astype(dtype)


def setup_inputs(seed: int = 0) -> dict:
    seeds = jax.random.split(jax.random.key(seed), 6)
    tokens = noise(seeds[0], (TOKENS, D), D ** -0.5, 0.125, ((0, 256),))
    target = noise(seeds[1], (TOKENS, FF), 1.0, 6.0, ((0, 32), (1, 8)))
    post_mean = noise(seeds[2], (D, FF), 1.0, 5.0, ((0, 32), (1, 8)), jnp.float32)
    post_hess = jnp.clip(jnp.exp(math.log(0.5) - 2.3025851 * jax.random.uniform(seeds[3], (D, FF), jnp.float32) ** shard_levels(seeds[3], (D, FF), ((0, 32), (1, 8)), -0.2, 0.2)), 0.05, 0.5)
    weight_noise = noise(seeds[4], (GROUPS, D, FF), 1.0, 6.0, ((1, 32), (2, 8)))
    return dict(tokens=tokens, target=target, post_mean=post_mean, post_hess=post_hess, weight_noise=weight_noise)


sample_size = 50.0
weight_decay = 0.02
hess_decay = 0.95
learn_rate = 0.3

def reference(tokens, target, post_mean, post_hess, weight_noise):
    post_std = lax.rsqrt(sample_size * (post_hess + weight_decay))
    token_groups = tokens.reshape(GROUPS, TOK_GRP, D)
    target_groups = target.reshape(GROUPS, TOK_GRP, FF)

    def one_group(totals, inputs):
        grad_sum, cross_sum = totals
        group_x, group_t, group_noise = inputs
        noise_vals = group_noise.astype(jnp.float32)
        sample = (post_mean + post_std * noise_vals).astype(jnp.bfloat16)
        output = jnp.dot(group_x, sample, preferred_element_type=jnp.float32)
        residual = (output - group_t.astype(jnp.float32)).astype(jnp.bfloat16)
        gradient = jnp.dot(group_x.T, residual, preferred_element_type=jnp.float32).astype(jnp.bfloat16)
        gradient = lax.optimization_barrier(gradient).astype(jnp.float32)
        return ((grad_sum + gradient, cross_sum + gradient * noise_vals), None)
    empty_sum = jnp.zeros((D, FF), jnp.float32)
    (grad_sum, cross_sum), _ = lax.scan(one_group, (empty_sum, empty_sum), (token_groups, target_groups, weight_noise))
    mean_grad = grad_sum / GROUPS
    hess_est = cross_sum / GROUPS / post_std
    keep_rate = 1.0 - hess_decay
    gap = post_hess - hess_est
    new_hess = hess_decay * post_hess + keep_rate * hess_est + 0.5 * keep_rate * keep_rate * gap * gap / (post_hess + weight_decay)
    new_mean = post_mean - learn_rate * (mean_grad + weight_decay * post_mean) / (new_hess + weight_decay)
    return (new_mean, new_hess)
```

```python
import jax
import jax.numpy as jnp
from jax import lax
from jax.sharding import PartitionSpec as P

sample_size = 50.0
weight_decay = 0.02
hess_decay = 0.95
learn_rate = 0.3


def contract_rows(left, right):
    return lax.dot_general(
        left, right, (((0,), (0,)), ((), ())), preferred_element_type=jnp.float32
    )


def local(tokens, target, post_mean, post_hess, weight_noise):
    groups = weight_noise.shape[0]
    post_std = lax.rsqrt(sample_size * (post_hess + weight_decay))
    noise_vals = weight_noise.astype(jnp.float32)
    samples = (post_mean[None] + post_std[None] * noise_vals).astype(jnp.bfloat16)
    group_x = lax.all_gather(tokens, "shard", axis=0, tiled=True)
    my_sample = lax.all_to_all(samples, "grp", split_axis=0, concat_axis=0, tiled=True)
    output = jnp.dot(
        group_x,
        my_sample.reshape(-1, my_sample.shape[-1]),
        preferred_element_type=jnp.float32,
    )
    residual = (output - target.astype(jnp.float32)).astype(jnp.bfloat16)
    gradient = contract_rows(group_x, residual).astype(jnp.bfloat16)
    group_grads = lax.all_to_all(
        gradient.reshape(samples.shape), "grp", split_axis=0, concat_axis=0, tiled=True
    )
    group_grads = group_grads.astype(jnp.float32)
    mean_grad = jnp.sum(group_grads, axis=0) / groups
    hess_est = jnp.sum(group_grads * noise_vals, axis=0) / groups / post_std
    keep_rate = 1.0 - hess_decay
    gap = post_hess - hess_est
    new_hess = (
        hess_decay * post_hess
        + keep_rate * hess_est
        + 0.5 * keep_rate * keep_rate * gap * gap / (post_hess + weight_decay)
    )
    new_mean = post_mean - learn_rate * (mean_grad + weight_decay * post_mean) / (
        new_hess + weight_decay
    )
    return (new_mean, new_hess)


def solution(mesh):
    return jax.shard_map(
        local,
        mesh=mesh,
        in_specs=(
            P(("grp", "shard"), None),
            P("grp", "shard"),
            P("grp", "shard"),
            P("grp", "shard"),
            P(None, "grp", "shard"),
        ),
        out_specs=(P("grp", "shard"), P("grp", "shard")),
        check_vma=False,
    )
```

```python
import jax
import jax.numpy as jnp
from jax import lax
from jax.sharding import PartitionSpec as P

sample_size = 50.0
weight_decay = 0.02
hess_decay = 0.95
learn_rate = 0.3


def contract_rows(left, right):
    return lax.dot_general(
        left, right, (((0,), (0,)), ((), ())), preferred_element_type=jnp.float32
    )


def column_chunks(width):
    first = min(width, ((width // 2 + 127) // 128) * 128)
    return [(0, first), (first, width)] if first < width else [(0, width)]


def local(tokens, target, post_mean, post_hess, weight_noise):
    groups = weight_noise.shape[0]
    post_std = lax.rsqrt(sample_size * (post_hess + weight_decay))
    group_x = lax.all_gather(tokens, "shard", axis=0, tiled=True)
    chunks = column_chunks(weight_noise.shape[-1])
    my_samples = []
    for lo, hi in chunks:
        noise_vals = weight_noise[:, :, lo:hi].astype(jnp.float32)
        samples = (post_mean[None, :, lo:hi] + post_std[None, :, lo:hi] * noise_vals).astype(
            jnp.bfloat16
        )
        my_samples.append(lax.all_to_all(samples, "grp", split_axis=0, concat_axis=0, tiled=True))
    grads = []
    for (lo, hi), my_sample in zip(chunks, my_samples):
        output = jnp.dot(
            group_x,
            my_sample.reshape(-1, hi - lo),
            preferred_element_type=jnp.float32,
        )
        residual = (output - target[:, lo:hi].astype(jnp.float32)).astype(jnp.bfloat16)
        gradient = contract_rows(group_x, residual).astype(jnp.bfloat16)
        grads.append(
            lax.all_to_all(
                gradient.reshape(my_sample.shape), "grp", split_axis=0, concat_axis=0, tiled=True
            )
        )
    group_grads = jnp.concatenate(grads, axis=-1).astype(jnp.float32)
    noise_vals = weight_noise.astype(jnp.float32)
    mean_grad = jnp.sum(group_grads, axis=0) / groups
    hess_est = jnp.sum(group_grads * noise_vals, axis=0) / groups / post_std
    keep_rate = 1.0 - hess_decay
    gap = post_hess - hess_est
    new_hess = (
        hess_decay * post_hess
        + keep_rate * hess_est
        + 0.5 * keep_rate * keep_rate * gap * gap / (post_hess + weight_decay)
    )
    new_mean = post_mean - learn_rate * (mean_grad + weight_decay * post_mean) / (
        new_hess + weight_decay
    )
    return (new_mean, new_hess)


def solution(mesh):
    return jax.shard_map(
        local,
        mesh=mesh,
        in_specs=(
            P(("grp", "shard"), None),
            P("grp", "shard"),
            P("grp", "shard"),
            P("grp", "shard"),
            P(None, "grp", "shard"),
        ),
        out_specs=(P("grp", "shard"), P("grp", "shard")),
        check_vma=False,
    )
```

```python
import jax
import jax.numpy as jnp
from jax import lax
from jax.sharding import Mesh, PartitionSpec as P

sample_size = 50.0
weight_decay = 0.02
hess_decay = 0.95
learn_rate = 0.3
Z_LINE = 4


def contract_rows(left, right):
    return lax.dot_general(
        left, right, (((0,), (0,)), ((), ())), preferred_element_type=jnp.float32
    )


def column_chunks(width):
    first = min(width, ((width // 2 + 127) // 128) * 128)
    return [(0, first), (first, width)] if first < width else [(0, width)]


def local(tokens, target, post_mean, post_hess, weight_noise):
    groups, rows, width = weight_noise.shape
    nz = Z_LINE
    nxc = groups // nz
    me = lax.axis_index("zl")
    post_std = lax.rsqrt(sample_size * (post_hess + weight_decay))
    group_x = lax.all_gather(tokens, "shard", axis=0, tiled=True)
    doubled = jnp.concatenate([group_x, group_x], axis=1)
    plane = group_x.shape[1] // nz
    x_r = lax.dynamic_slice_in_dim(doubled, me * plane, group_x.shape[1], axis=1)
    chunks = column_chunks(width)
    staged = []
    for lo, hi in chunks:
        noise_vals = weight_noise[:, :, lo:hi].astype(jnp.float32)
        samples = (post_mean[None, :, lo:hi] + post_std[None, :, lo:hi] * noise_vals).astype(
            jnp.bfloat16
        )
        s4 = samples.reshape(nz, nxc, rows, hi - lo)
        staged.append(lax.all_to_all(s4, "xc", split_axis=1, concat_axis=1, tiled=True))
    grads = []
    for (lo, hi), t1 in zip(chunks, staged):
        blocks = [t1[me]]
        for e in range(1, nz):
            part = lax.dynamic_index_in_dim(t1, (me - e) % nz, axis=0, keepdims=False)
            perm = [(src, (src - e) % nz) for src in range(nz)]
            blocks.append(lax.ppermute(part, "zl", perm))
        full = jnp.stack(blocks).reshape(-1, hi - lo)
        output = jnp.dot(x_r, full, preferred_element_type=jnp.float32)
        residual = (output - target[:, lo:hi].astype(jnp.float32)).astype(jnp.bfloat16)
        grad_r = contract_rows(x_r, residual).astype(jnp.bfloat16).reshape(nz, nxc, rows, hi - lo)
        back = [grad_r[0]]
        for e in range(1, nz):
            perm = [(src, (src + e) % nz) for src in range(nz)]
            back.append(lax.ppermute(grad_r[e], "zl", perm))
        q = jnp.stack(back)
        grads.append(lax.all_to_all(q, "xc", split_axis=1, concat_axis=1, tiled=True))
    group_grads = jnp.concatenate(grads, axis=-1).astype(jnp.float32)
    order = (me - jnp.arange(nz)) % nz
    noise_r = jnp.take(weight_noise.reshape(nz, nxc, rows, width), order, axis=0)
    mean_grad = jnp.sum(group_grads, axis=(0, 1)) / groups
    hess_est = (
        jnp.sum(group_grads * noise_r.astype(jnp.float32), axis=(0, 1)) / groups / post_std
    )
    keep_rate = 1.0 - hess_decay
    gap = post_hess - hess_est
    new_hess = (
        hess_decay * post_hess
        + keep_rate * hess_est
        + 0.5 * keep_rate * keep_rate * gap * gap / (post_hess + weight_decay)
    )
    new_mean = post_mean - learn_rate * (mean_grad + weight_decay * post_mean) / (
        new_hess + weight_decay
    )
    return (new_mean, new_hess)


def solution(mesh):
    n_grp = mesh.shape["grp"]
    fine = Mesh(
        mesh.devices.reshape(Z_LINE, n_grp // Z_LINE, mesh.shape["shard"]),
        ("zl", "xc", "shard"),
    )
    grp = ("zl", "xc")
    return jax.shard_map(
        local,
        mesh=fine,
        in_specs=(
            P(("zl", "xc", "shard"), None),
            P(grp, "shard"),
            P(grp, "shard"),
            P(grp, "shard"),
            P(None, grp, "shard"),
        ),
        out_specs=(P(grp, "shard"), P(grp, "shard")),
        check_vma=False,
    )
```

```python
import jax
import jax.numpy as jnp
from jax import lax
from jax.sharding import PartitionSpec as P

sample_size = 50.0
weight_decay = 0.02
hess_decay = 0.95
learn_rate = 0.3


def contract_rows(left, right):
    return lax.dot_general(
        left, right, (((0,), (0,)), ((), ())), preferred_element_type=jnp.float32
    )


def column_chunks(width):
    first = min(width, ((width // 2 + 127) // 128) * 128)
    return [(0, first), (first, width)] if first < width else [(0, width)]


def exchange_by_permutes(blocks, axis, n, me, outward):
    got = [lax.dynamic_index_in_dim(blocks, me, axis=0, keepdims=False) if not outward else blocks[0]]
    for d in range(1, n):
        if outward:
            part = blocks[d]
            perm = [(i, (i + d) % n) for i in range(n)]
        else:
            part = lax.dynamic_index_in_dim(blocks, (me - d) % n, axis=0, keepdims=False)
            perm = [(i, (i - d) % n) for i in range(n)]
        got.append(lax.ppermute(part, axis, perm))
    return jnp.stack(got)


def local(tokens, target, post_mean, post_hess, weight_noise):
    groups, rows, width = weight_noise.shape
    me = lax.axis_index("grp")
    post_std = lax.rsqrt(sample_size * (post_hess + weight_decay))
    group_x = lax.all_gather(tokens, "shard", axis=0, tiled=True)
    doubled = jnp.concatenate([group_x, group_x], axis=1)
    x_r = lax.dynamic_slice_in_dim(doubled, me * rows, group_x.shape[1], axis=1)
    chunks = column_chunks(width)
    via_permutes = [i == len(chunks) - 1 and len(chunks) > 1 for i in range(len(chunks))]
    my_samples = []
    for (lo, hi), perm_path in zip(chunks, via_permutes):
        noise_vals = weight_noise[:, :, lo:hi].astype(jnp.float32)
        samples = (post_mean[None, :, lo:hi] + post_std[None, :, lo:hi] * noise_vals).astype(
            jnp.bfloat16
        )
        if perm_path:
            my_samples.append(exchange_by_permutes(samples, "grp", groups, me, False))
        else:
            my_samples.append(
                lax.all_to_all(samples, "grp", split_axis=0, concat_axis=0, tiled=True)
            )
    means, hesses = [], []
    for (lo, hi), perm_path, my_sample in zip(chunks, via_permutes, my_samples):
        xs = x_r if perm_path else group_x
        output = jnp.dot(xs, my_sample.reshape(-1, hi - lo), preferred_element_type=jnp.float32)
        residual = (output - target[:, lo:hi].astype(jnp.float32)).astype(jnp.bfloat16)
        gradient = contract_rows(xs, residual).astype(jnp.bfloat16).reshape(my_sample.shape)
        noise_c = weight_noise[:, :, lo:hi]
        if perm_path:
            group_grads = exchange_by_permutes(gradient, "grp", groups, me, True)
            order = (me - jnp.arange(groups)) % groups
            noise_c = jnp.take(noise_c, order, axis=0)
        else:
            group_grads = lax.all_to_all(gradient, "grp", split_axis=0, concat_axis=0, tiled=True)
        group_grads = group_grads.astype(jnp.float32)
        means.append(jnp.sum(group_grads, axis=0))
        hesses.append(jnp.sum(group_grads * noise_c.astype(jnp.float32), axis=0))
    mean_grad = jnp.concatenate(means, axis=-1) / groups
    hess_est = jnp.concatenate(hesses, axis=-1) / groups / post_std
    keep_rate = 1.0 - hess_decay
    gap = post_hess - hess_est
    new_hess = (
        hess_decay * post_hess
        + keep_rate * hess_est
        + 0.5 * keep_rate * keep_rate * gap * gap / (post_hess + weight_decay)
    )
    new_mean = post_mean - learn_rate * (mean_grad + weight_decay * post_mean) / (
        new_hess + weight_decay
    )
    return (new_mean, new_hess)


def solution(mesh):
    return jax.shard_map(
        local,
        mesh=mesh,
        in_specs=(
            P(("grp", "shard"), None),
            P("grp", "shard"),
            P("grp", "shard"),
            P("grp", "shard"),
            P(None, "grp", "shard"),
        ),
        out_specs=(P("grp", "shard"), P("grp", "shard")),
        check_vma=False,
    )
```

```python
import jax
import jax.numpy as jnp
from jax import lax
from jax.sharding import PartitionSpec as P

sample_size = 50.0
weight_decay = 0.02
hess_decay = 0.95
learn_rate = 0.3


def contract_rows(left, right):
    return lax.dot_general(
        left, right, (((0,), (0,)), ((), ())), preferred_element_type=jnp.float32
    )


def column_chunks(width):
    first = min(width, ((width // 2 + 127) // 128) * 128)
    return [(0, first), (first, width)] if first < width else [(0, width)]


def local(tokens, target, post_mean, post_hess, weight_noise):
    groups = weight_noise.shape[0]
    post_std = lax.rsqrt(sample_size * (post_hess + weight_decay))
    group_x = lax.all_gather(tokens, "shard", axis=0, tiled=True)
    chunks = column_chunks(weight_noise.shape[-1])
    my_samples = []
    for lo, hi in chunks:
        noise_vals = weight_noise[:, :, lo:hi].astype(jnp.float32)
        samples = (post_mean[None, :, lo:hi] + post_std[None, :, lo:hi] * noise_vals).astype(
            jnp.bfloat16
        )
        my_samples.append(lax.all_to_all(samples, "grp", split_axis=0, concat_axis=0, tiled=True))
    means, hesses = [], []
    for (lo, hi), my_sample in zip(chunks, my_samples):
        output = jnp.dot(
            group_x,
            my_sample.reshape(-1, hi - lo),
            preferred_element_type=jnp.float32,
        )
        residual = (output - target[:, lo:hi].astype(jnp.float32)).astype(jnp.bfloat16)
        gradient = contract_rows(group_x, residual).astype(jnp.bfloat16)
        group_grads = lax.all_to_all(
            gradient.reshape(my_sample.shape), "grp", split_axis=0, concat_axis=0, tiled=True
        ).astype(jnp.float32)
        pm = post_mean[:, lo:hi]
        ph = post_hess[:, lo:hi]
        mean_grad = jnp.sum(group_grads, axis=0) / groups
        hess_est = (
            jnp.sum(group_grads * weight_noise[:, :, lo:hi].astype(jnp.float32), axis=0)
            / groups
            / post_std[:, lo:hi]
        )
        keep_rate = 1.0 - hess_decay
        gap = ph - hess_est
        new_hess = (
            hess_decay * ph
            + keep_rate * hess_est
            + 0.5 * keep_rate * keep_rate * gap * gap / (ph + weight_decay)
        )
        new_mean = pm - learn_rate * (mean_grad + weight_decay * pm) / (new_hess + weight_decay)
        means.append(new_mean)
        hesses.append(new_hess)
    new_mean = jnp.concatenate(means, axis=-1)
    new_hess = jnp.concatenate(hesses, axis=-1)
    return (new_mean, new_hess)


def solution(mesh):
    return jax.shard_map(
        local,
        mesh=mesh,
        in_specs=(
            P(("grp", "shard"), None),
            P("grp", "shard"),
            P("grp", "shard"),
            P("grp", "shard"),
            P(None, "grp", "shard"),
        ),
        out_specs=(P("grp", "shard"), P("grp", "shard")),
        check_vma=False,
    )
```

```python
import jax
import jax.numpy as jnp
from jax import lax
from jax.sharding import PartitionSpec as P

sample_size = 50.0
weight_decay = 0.02
hess_decay = 0.95
learn_rate = 0.3


def contract_rows(left, right):
    return lax.dot_general(
        left, right, (((0,), (0,)), ((), ())), preferred_element_type=jnp.float32
    )


def column_chunks(width):
    first = min(width, ((width // 2 + 127) // 128) * 128)
    return [(0, first), (first, width)] if first < width else [(0, width)]


def local(tokens, target, post_mean, post_hess, weight_noise):
    groups = weight_noise.shape[0]
    post_std = lax.rsqrt(sample_size * (post_hess + weight_decay))
    n_shard = lax.axis_size("shard")
    me_s = lax.axis_index("shard")
    blocks = [tokens] + [
        lax.ppermute(tokens, "shard", [(i, (i - d) % n_shard) for i in range(n_shard)])
        for d in range(1, n_shard)
    ]
    doubled = jnp.concatenate(blocks + blocks, axis=0)
    group_x = lax.dynamic_slice_in_dim(
        doubled, ((n_shard - me_s) % n_shard) * tokens.shape[0], n_shard * tokens.shape[0], axis=0
    )
    chunks = column_chunks(weight_noise.shape[-1])
    my_samples = []
    for lo, hi in chunks:
        noise_vals = weight_noise[:, :, lo:hi].astype(jnp.float32)
        samples = (post_mean[None, :, lo:hi] + post_std[None, :, lo:hi] * noise_vals).astype(
            jnp.bfloat16
        )
        my_samples.append(lax.all_to_all(samples, "grp", split_axis=0, concat_axis=0, tiled=True))
    means, hesses = [], []
    for (lo, hi), my_sample in zip(chunks, my_samples):
        output = jnp.dot(
            group_x,
            my_sample.reshape(-1, hi - lo),
            preferred_element_type=jnp.float32,
        )
        residual = (output - target[:, lo:hi].astype(jnp.float32)).astype(jnp.bfloat16)
        gradient = contract_rows(group_x, residual).astype(jnp.bfloat16)
        group_grads = lax.all_to_all(
            gradient.reshape(my_sample.shape), "grp", split_axis=0, concat_axis=0, tiled=True
        ).astype(jnp.float32)
        pm = post_mean[:, lo:hi]
        ph = post_hess[:, lo:hi]
        mean_grad = jnp.sum(group_grads, axis=0) / groups
        hess_est = (
            jnp.sum(group_grads * weight_noise[:, :, lo:hi].astype(jnp.float32), axis=0)
            / groups
            / post_std[:, lo:hi]
        )
        keep_rate = 1.0 - hess_decay
        gap = ph - hess_est
        new_hess = (
            hess_decay * ph
            + keep_rate * hess_est
            + 0.5 * keep_rate * keep_rate * gap * gap / (ph + weight_decay)
        )
        new_mean = pm - learn_rate * (mean_grad + weight_decay * pm) / (new_hess + weight_decay)
        means.append(new_mean)
        hesses.append(new_hess)
    new_mean = jnp.concatenate(means, axis=-1)
    new_hess = jnp.concatenate(hesses, axis=-1)
    return (new_mean, new_hess)


def solution(mesh):
    return jax.shard_map(
        local,
        mesh=mesh,
        in_specs=(
            P(("grp", "shard"), None),
            P("grp", "shard"),
            P("grp", "shard"),
            P("grp", "shard"),
            P(None, "grp", "shard"),
        ),
        out_specs=(P("grp", "shard"), P("grp", "shard")),
        check_vma=False,
    )
```

```python
import jax
import jax.numpy as jnp
from jax import lax
from jax.sharding import PartitionSpec as P


sample_size = 50.0
weight_decay = 0.02
hess_decay = 0.95
learn_rate = 0.3


def contract_rows(left, right):
    return lax.dot_general(
        left, right, (((0,), (0,)), ((), ())), preferred_element_type=jnp.float32
    )


def column_chunks(width):
    first = min(width, ((width // 2 + 127) // 128) * 128)
    return [(0, first), (first, width)] if first < width else [(0, width)]


def local(tokens, target, post_mean, post_hess, weight_noise):
    groups = weight_noise.shape[0]
    post_std = lax.rsqrt(sample_size * (post_hess + weight_decay))
    half = tokens.shape[1] // 2
    x_a = lax.all_gather(tokens[:, :half], "shard", axis=0, tiled=True)
    x_b = lax.all_gather(tokens[:, half:], "shard", axis=0, tiled=True)
    group_x = jnp.concatenate([x_a, x_b], axis=1)
    chunks = column_chunks(weight_noise.shape[-1])
    my_samples = []
    for lo, hi in chunks:
        noise_vals = weight_noise[:, :, lo:hi].astype(jnp.float32)
        samples = (post_mean[None, :, lo:hi] + post_std[None, :, lo:hi] * noise_vals).astype(
            jnp.bfloat16
        )
        my_samples.append(lax.all_to_all(samples, "grp", split_axis=0, concat_axis=0, tiled=True))
    means, hesses = [], []
    for (lo, hi), my_sample in zip(chunks, my_samples):
        output = jnp.dot(
            group_x,
            my_sample.reshape(-1, hi - lo),
            preferred_element_type=jnp.float32,
        )
        residual = (output - target[:, lo:hi].astype(jnp.float32)).astype(jnp.bfloat16)
        gradient = contract_rows(group_x, residual).astype(jnp.bfloat16)
        group_grads = lax.all_to_all(
            gradient.reshape(my_sample.shape), "grp", split_axis=0, concat_axis=0, tiled=True
        ).astype(jnp.float32)
        pm = post_mean[:, lo:hi]
        ph = post_hess[:, lo:hi]
        mean_grad = jnp.sum(group_grads, axis=0) / groups
        hess_est = (
            jnp.sum(group_grads * weight_noise[:, :, lo:hi].astype(jnp.float32), axis=0)
            / groups
            / post_std[:, lo:hi]
        )
        keep_rate = 1.0 - hess_decay
        gap = ph - hess_est
        new_hess = (
            hess_decay * ph
            + keep_rate * hess_est
            + 0.5 * keep_rate * keep_rate * gap * gap / (ph + weight_decay)
        )
        new_mean = pm - learn_rate * (mean_grad + weight_decay * pm) / (new_hess + weight_decay)
        means.append(new_mean)
        hesses.append(new_hess)
    new_mean = jnp.concatenate(means, axis=-1)
    new_hess = jnp.concatenate(hesses, axis=-1)
    return (new_mean, new_hess)


def solution(mesh):
    return jax.shard_map(
        local,
        mesh=mesh,
        in_specs=(
            P(("grp", "shard"), None),
            P("grp", "shard"),
            P("grp", "shard"),
            P("grp", "shard"),
            P(None, "grp", "shard"),
        ),
        out_specs=(P("grp", "shard"), P("grp", "shard")),
        check_vma=False,
    )
```

```python
import jax
import jax.numpy as jnp
from jax import lax
from jax.sharding import Mesh, PartitionSpec as P

sample_size = 50.0
weight_decay = 0.02
hess_decay = 0.95
learn_rate = 0.3


def contract_rows(left, right):
    return lax.dot_general(
        left, right, (((0,), (0,)), ((), ())), preferred_element_type=jnp.float32
    )


def column_chunks(width):
    first = min(width, ((width // 2 + 127) // 128) * 128)
    return [(0, first), (first, width)] if first < width else [(0, width)]


def local(tokens, target, post_mean, post_hess, weight_noise):
    groups = weight_noise.shape[0]
    post_std = lax.rsqrt(sample_size * (post_hess + weight_decay))
    pair = lax.all_gather(tokens, "zh", axis=0, tiled=False)
    quad = lax.all_gather(pair, "y", axis=0, tiled=False)
    group_x = jnp.swapaxes(quad, 0, 1).reshape(-1, tokens.shape[1])
    chunks = column_chunks(weight_noise.shape[-1])
    my_samples = []
    for lo, hi in chunks:
        noise_vals = weight_noise[:, :, lo:hi].astype(jnp.float32)
        samples = (post_mean[None, :, lo:hi] + post_std[None, :, lo:hi] * noise_vals).astype(
            jnp.bfloat16
        )
        my_samples.append(lax.all_to_all(samples, "grp", split_axis=0, concat_axis=0, tiled=True))
    means, hesses = [], []
    for (lo, hi), my_sample in zip(chunks, my_samples):
        output = jnp.dot(
            group_x,
            my_sample.reshape(-1, hi - lo),
            preferred_element_type=jnp.float32,
        )
        residual = (output - target[:, lo:hi].astype(jnp.float32)).astype(jnp.bfloat16)
        gradient = contract_rows(group_x, residual).astype(jnp.bfloat16)
        group_grads = lax.all_to_all(
            gradient.reshape(my_sample.shape), "grp", split_axis=0, concat_axis=0, tiled=True
        ).astype(jnp.float32)
        pm = post_mean[:, lo:hi]
        ph = post_hess[:, lo:hi]
        mean_grad = jnp.sum(group_grads, axis=0) / groups
        hess_est = (
            jnp.sum(group_grads * weight_noise[:, :, lo:hi].astype(jnp.float32), axis=0)
            / groups
            / post_std[:, lo:hi]
        )
        keep_rate = 1.0 - hess_decay
        gap = ph - hess_est
        new_hess = (
            hess_decay * ph
            + keep_rate * hess_est
            + 0.5 * keep_rate * keep_rate * gap * gap / (ph + weight_decay)
        )
        new_mean = pm - learn_rate * (mean_grad + weight_decay * pm) / (new_hess + weight_decay)
        means.append(new_mean)
        hesses.append(new_hess)
    new_mean = jnp.concatenate(means, axis=-1)
    new_hess = jnp.concatenate(hesses, axis=-1)
    return (new_mean, new_hess)


def solution(mesh):
    n_shard = mesh.shape["shard"]
    fine = Mesh(
        mesh.devices.reshape(mesh.shape["grp"], 2, n_shard // 2), ("grp", "zh", "y")
    )
    shard = ("zh", "y")
    return jax.shard_map(
        local,
        mesh=fine,
        in_specs=(
            P(("grp", "zh", "y"), None),
            P("grp", shard),
            P("grp", shard),
            P("grp", shard),
            P(None, "grp", shard),
        ),
        out_specs=(P("grp", shard), P("grp", shard)),
        check_vma=False,
    )
```
